32 devices in a mesh: seq: 8 (over z, y), ch: 4 (over x, core).
Axes of the slice: x: 2, y: 2, z: 4, core: 2. Of those that a mesh axis runs over, the one named last changes fastest.
Arguments:
- inputs: bfloat16 [1024, 4096], P('seq', 'ch'), may hold values from -6 to 6
- gate_values: bfloat16 [1024, 4096], P('seq', 'ch'), may hold values from -6 to 6
- grad_out: bfloat16 [1024, 4096], P('seq', 'ch'), may hold values from -6 to 6
- first_weight: float32 [32, 256], replicated, may hold values from -4 to 4
- first_bias: float32 [256], replicated, may hold values from -3.140625 to 3.140625
- second_weight: float32 [256, 256], replicated, may hold values from -0.75 to 0.75
- second_bias: float32 [256], replicated, may hold values from -3.140625 to 3.140625
- out_weight: float32 [256, 4096], P(None, 'ch'), may hold values from -0.0546875 to 0.0546875
- decay_rates: float32 [4096], P('ch'), as said below
- mask_lengths: int32 [4096], P('ch'), may hold values from 1 to 512, as said below
Outputs:
- grad_inputs: bfloat16 [1024, 4096], P('seq', 'ch')
- grad_gates: bfloat16 [1024, 4096], P('seq', 'ch')
- grad_first_weight: float32 [32, 256], replicated
- grad_first_bias: float32 [256], replicated
- grad_second_weight: float32 [256, 256], replicated
- grad_second_bias: float32 [256], replicated
- grad_out_weight: float32 [256, 4096], P(None, 'ch')
The draws below stay inside these ranges and needn't reach their ends.
Inputs may be any that keep to these rules, and one draw needn't show every extreme that they name: `mask_lengths`: each channel's decay-mask length in lags; in every aligned group of 32 channels at least one channel has exactly 512. `decay_rates`: positive decay rates between 1 / 5120 and 1 / 40.
All inputs are finite; a program needn't handle non-finite values.
Results may differ from the reference program's by a relative error of at most 0.013.
Values may be sent and summed in bfloat16 or wider, within the bound.
A program may use at most 128 MiB of HBM per device.

```python
import math
import jax
import jax.numpy as jnp
from jax import lax

D = 4096
FW = 256
EMB = 32
WIN = 512
TOKENS = 1024


def draw_decay_rates(key, part):
    key_slow = jax.random.fold_in(key, 0)
    lowest = math.log(0.1 / WIN)
    highest = math.log(1.0 / 40.0)
    spread = jax.random.uniform(key_slow, (D,), jnp.float32, lowest, highest)
    return jnp.exp(spread).astype(jnp.float32)


def draw_mask_lengths(key, part):
    key_base, key_spot = jax.random.split(key)
    base_lengths = jax.random.randint(key_base, (D,), 1, WIN + 1, dtype=jnp.int32)
    groups = D // 32
    chosen_slot = jax.random.randint(key_spot, (groups, 1), 0, 32, dtype=jnp.int32)
    hitting = jnp.arange(32, dtype=jnp.int32)[None, :] == chosen_slot
    return jnp.where(hitting.reshape(D), WIN, base_lengths).astype(jnp.int32)


def levels(key, dims, pieces, low, largest):
    def one(axis_at, blocks):
        steps = jax.random.uniform(jax.random.fold_in(jax.random.fold_in(key, 6), axis_at), (blocks,), jnp.float32, low / len(pieces), largest / len(pieces))
        return jnp.repeat(jnp.exp(steps), dims[axis_at] // blocks).reshape((-1,) + (1,) * (len(dims) - axis_at - 1))

    level = one(*pieces[0])
    for cut in pieces[1:]:
        level = level * one(*cut)
    return level


def bell_draw(stream_key, dims, scale, reach, cuts=(), kind=jnp.bfloat16):
    gain = levels(stream_key, dims, cuts, -0.22, 0.18) if cuts else 1.0
    drawn = jax.random.normal(stream_key, dims, jnp.float32) * scale * gain
    return jnp.minimum(jnp.maximum(drawn, -reach), reach).astype(kind)


def setup_inputs(seed: int = 0) -> dict:
    splits = jax.random.split(jax.random.key(seed), 11)
    return {
        "inputs": bell_draw(splits[0], (TOKENS, D), 1.0, 6.0, ((0, 8), (1, 4))),
        "gate_values": bell_draw(splits[1], (TOKENS, D), 1.0, 6.0, ((0, 8), (1, 4))),
        "grad_out": bell_draw(splits[2], (TOKENS, D), 1.0, 6.0, ((0, 8), (1, 4))),
        "first_weight": bell_draw(splits[3], (EMB, FW), 1.0, 4.0, (), jnp.float32),
        "first_bias": jnp.clip(jax.random.uniform(splits[4], (FW,), jnp.float32, -3.140625, 3.140625), -3.140625, 3.140625),
        "second_weight": bell_draw(splits[5], (FW, FW), (FW // 4) ** -0.5, 0.75, (), jnp.float32),
        "second_bias": jnp.clip(jax.random.uniform(splits[6], (FW,), jnp.float32, -3.140625, 3.140625), -3.140625, 3.140625),
        "out_weight": bell_draw(splits[7], (FW, D), (FW * WIN // 10) ** -0.5, 0.0546875, ((1, 4),), jnp.float32),
        "decay_rates": draw_decay_rates(jax.random.fold_in(splits[10], 71), 0),
        "mask_lengths": draw_mask_lengths(jax.random.fold_in(splits[10], 71), 0),
    }


FULL_PRECISION = lax.Precision.HIGHEST

def angle_table(first_index, second_index, period):
    product = first_index[:, None] * second_index[None, :] % period
    return 2.0 * math.pi / period * product.astype(jnp.float32)

def lag_features(lag_count, feature_count):
    lag_index = jnp.arange(lag_count, dtype=jnp.int32)
    band_index = jnp.arange(feature_count // 2, dtype=jnp.int32) + 1
    phases = angle_table(lag_index, band_index, 2 * feature_count)
    return jnp.concatenate([jnp.cos(phases), jnp.sin(phases)], axis=1)

def reference(inputs, gate_values, grad_out, first_weight, first_bias, second_weight, second_bias, out_weight, decay_rates, mask_lengths):
    features = lag_features(WIN, EMB)
    pre_first = jnp.dot(features, first_weight, precision=FULL_PRECISION) + first_bias
    hidden_one = jnp.sin(pre_first)
    pre_second = jnp.dot(hidden_one, second_weight, precision=FULL_PRECISION) + second_bias
    hidden_two = jnp.sin(pre_second)
    lag_index = jnp.arange(WIN, dtype=jnp.int32)
    envelope = jnp.exp(-decay_rates[None, :] * lag_index.astype(jnp.float32)[:, None]) * (lag_index[:, None] < mask_lengths[None, :]).astype(jnp.float32)
    filter_taps = jnp.dot(hidden_two, out_weight, precision=FULL_PRECISION) * envelope
    padded_taps = jnp.pad(filter_taps, ((0, TOKENS - WIN), (0, 0)))
    taps_spectrum = jnp.fft.rfft(padded_taps, axis=0)
    input_spectrum = jnp.fft.rfft(inputs.astype(jnp.float32), axis=0)
    convolved = jnp.fft.irfft(taps_spectrum * input_spectrum, n=TOKENS, axis=0).astype(jnp.float32)
    grad_gates = (grad_out.astype(jnp.float32) * convolved).astype(jnp.bfloat16)
    carried = (grad_out.astype(jnp.float32) * gate_values.astype(jnp.float32)).astype(jnp.bfloat16)
    carried = lax.optimization_barrier(carried).astype(jnp.float32)
    carried_spectrum = jnp.fft.rfft(carried, axis=0)
    grad_inputs = jnp.fft.irfft(jnp.conj(taps_spectrum) * carried_spectrum, n=TOKENS, axis=0).astype(jnp.float32).astype(jnp.bfloat16)
    tap_sums = jnp.fft.irfft(carried_spectrum * jnp.conj(input_spectrum), n=TOKENS, axis=0)[:WIN].astype(jnp.float32)
    grad_taps = tap_sums * envelope * (1.0 / math.sqrt(TOKENS * WIN))
    grad_out_weight = jnp.dot(hidden_two.T, grad_taps, precision=FULL_PRECISION)
    grad_two = jnp.dot(grad_taps, out_weight.T, precision=FULL_PRECISION) * jnp.cos(pre_second)
    grad_second_weight = jnp.dot(hidden_one.T, grad_two, precision=FULL_PRECISION)
    grad_second_bias = lax.optimization_barrier(jnp.sum(grad_two, axis=0))
    grad_one = jnp.dot(grad_two, second_weight.T, precision=FULL_PRECISION) * jnp.cos(pre_first)
    grad_first_weight = jnp.dot(features.T, grad_one, precision=FULL_PRECISION)
    grad_first_bias = lax.optimization_barrier(jnp.sum(grad_one, axis=0))
    return (grad_inputs, grad_gates, grad_first_weight, grad_first_bias, grad_second_weight, grad_second_bias, grad_out_weight)
```

```python
import math

import jax
import jax.numpy as jnp
import functools

import numpy as np
from jax import lax
from jax.experimental import pallas as pl
from jax.experimental.pallas import tpu as pltpu
from jax.sharding import PartitionSpec as P

SPAN = 4


FULL_PRECISION = lax.Precision.HIGHEST


def passed_along(value, axis, steps):
    count = lax.axis_size(axis)
    pairs = [(source, (source + steps) % count) for source in range(count)]
    return lax.ppermute(value, axis, pairs)


def angle_table(first_index, second_index, period):
    product = first_index[:, None] * second_index[None, :] % period
    return 2.0 * math.pi / period * product.astype(jnp.float32)


def lag_features(lag_count, feature_count):
    lag_index = jnp.arange(lag_count, dtype=jnp.int32)
    band_index = jnp.arange(feature_count // 2, dtype=jnp.int32) + 1
    phases = angle_table(lag_index, band_index, 2 * feature_count)
    return jnp.concatenate([jnp.cos(phases), jnp.sin(phases)], axis=1)


def split_table(table):
    upper_part = table.astype(jnp.bfloat16)
    lower_part = (table - upper_part.astype(jnp.float32)).astype(jnp.bfloat16)
    return (upper_part, lower_part)


def transform_tables(shard_rows):
    period = 2 * shard_rows
    frequency = jnp.arange(shard_rows + 1, dtype=jnp.int32)
    position = jnp.arange(shard_rows, dtype=jnp.int32)
    bin_weight = jnp.where((frequency == 0) | (frequency == shard_rows), 1.0, 2.0).astype(
        jnp.float32
    )
    forward_angles = angle_table(frequency, position, period)
    mirror_angles = angle_table(frequency, shard_rows - 1 - position, period)
    back_angles = angle_table(position + shard_rows, frequency, period)
    mirror_back = angle_table(2 * shard_rows - 1 - position, frequency, period)
    front_table = jnp.stack([jnp.cos(forward_angles), -jnp.sin(forward_angles)])
    mirror_table = jnp.stack([jnp.cos(mirror_angles), -jnp.sin(mirror_angles)])
    back_plain = jnp.stack([jnp.cos(back_angles), -jnp.sin(back_angles)]) / period
    back_table = back_plain * bin_weight[None, None, :]
    mirror_out = jnp.stack([jnp.cos(mirror_back), -jnp.sin(mirror_back)]) * (
        bin_weight[None, None, :] / period
    )
    fold_table = front_table * bin_weight[None, :, None]
    parity = (1.0 - 2.0 * (frequency % 2).astype(jnp.float32))[None, :, None]
    return (front_table, mirror_table, back_plain, back_table, mirror_out, fold_table, parity)


def spectrum(table_in, signal):
    return jnp.einsum("kfs,sc->kfc", table_in, signal, precision=FULL_PRECISION)


def sample_spectrum(table_pair, signal):
    upper_term = jnp.einsum(
        "kfs,sc->kfc", table_pair[0], signal, preferred_element_type=jnp.float32
    )
    lower_term = jnp.einsum(
        "kfs,sc->kfc", table_pair[1], signal, preferred_element_type=jnp.float32
    )
    return upper_term + lower_term


def sample_pullback(table_pair, signal):
    upper_term = jnp.einsum(
        "ksf,sc->kfc", table_pair[0], signal, preferred_element_type=jnp.float32
    )
    lower_term = jnp.einsum(
        "ksf,sc->kfc", table_pair[1], signal, preferred_element_type=jnp.float32
    )
    return upper_term + lower_term


def complex_product(left_factor, right_factor):
    real_part = left_factor[0] * right_factor[0] - left_factor[1] * right_factor[1]
    imag_part = left_factor[0] * right_factor[1] + left_factor[1] * right_factor[0]
    return jnp.stack([real_part, imag_part])


def conjugate_product(left_factor, right_factor):
    real_part = left_factor[0] * right_factor[0] + left_factor[1] * right_factor[1]
    imag_part = left_factor[1] * right_factor[0] - left_factor[0] * right_factor[1]
    return jnp.stack([real_part, imag_part])


def weighted_sum(filter_mixes, spectra_items):
    accumulated = complex_product(filter_mixes[0], spectra_items[0])
    for offset in range(1, len(filter_mixes)):
        accumulated = accumulated + complex_product(filter_mixes[offset], spectra_items[offset])
    return accumulated


def per_device(
    inputs,
    gate_values,
    grad_out,
    first_weight,
    first_bias,
    second_weight,
    second_bias,
    out_weight,
    decay_rates,
    mask_lengths,
):
    shard_rows = inputs.shape[0]
    window = SPAN * shard_rows
    front_table, mirror_table, back_plain, back_table, mirror_out, fold_table, parity = (
        transform_tables(shard_rows)
    )
    front_pair = split_table(front_table)
    mirror_pair = split_table(mirror_table)
    pull_pair = split_table(back_plain)
    features = lag_features(window, first_weight.shape[0])
    pre_first = jnp.dot(features, first_weight, precision=FULL_PRECISION) + first_bias
    hidden_one = jnp.sin(pre_first)
    pre_second = jnp.dot(hidden_one, second_weight, precision=FULL_PRECISION) + second_bias
    hidden_two = jnp.sin(pre_second)
    lag_index = jnp.arange(window, dtype=jnp.int32)
    envelope = jnp.exp(-decay_rates[None, :] * lag_index.astype(jnp.float32)[:, None]) * (
        lag_index[:, None] < mask_lengths[None, :]
    ).astype(jnp.float32)
    filter_taps = jnp.dot(hidden_two, out_weight, precision=FULL_PRECISION) * envelope
    block_spectra = [
        spectrum(front_table, filter_taps[block * shard_rows : (block + 1) * shard_rows])
        for block in range(SPAN)
    ]
    filter_mixes = []
    for offset in range(SPAN + 1):
        if offset == 0:
            mixed = parity * block_spectra[0]
        elif offset == SPAN:
            mixed = block_spectra[SPAN - 1]
        else:
            mixed = block_spectra[offset - 1] + parity * block_spectra[offset]
        filter_mixes.append(mixed)
    carried = (grad_out.astype(jnp.float32) * gate_values.astype(jnp.float32)).astype(jnp.bfloat16)
    earlier_spectra = [sample_spectrum(front_pair, inputs)]
    later_spectra = [sample_spectrum(mirror_pair, carried)]
    for offset in range(1, SPAN + 1):
        earlier = passed_along(inputs, "seq", offset)
        later = passed_along(carried, "seq", -offset)
        earlier_spectra.append(sample_spectrum(front_pair, earlier))
        later_spectra.append(sample_spectrum(mirror_pair, later))
    convolved = jnp.einsum(
        "ksf,kfc->sc",
        back_table,
        weighted_sum(filter_mixes, earlier_spectra),
        precision=FULL_PRECISION,
    )
    grad_gates = (grad_out.astype(jnp.float32) * convolved).astype(jnp.bfloat16)
    grad_inputs = jnp.einsum(
        "ksf,kfc->sc",
        mirror_out,
        weighted_sum(filter_mixes, later_spectra),
        precision=FULL_PRECISION,
    ).astype(jnp.bfloat16)
    pulled = sample_pullback(pull_pair, carried)
    grad_mixes = [conjugate_product(pulled, spectra_item) for spectra_item in earlier_spectra]
    pieces = []
    for block in range(SPAN):
        grad_block = parity * grad_mixes[block] + grad_mixes[block + 1]
        pieces.append(jnp.einsum("kfs,kfc->sc", fold_table, grad_block, precision=FULL_PRECISION))
    tap_terms = jnp.concatenate(pieces, axis=0)
    grad_scale = 1.0 / math.sqrt(lax.axis_size("seq") * shard_rows * window)
    tap_sums = lax.psum(tap_terms, "seq")
    grad_taps = tap_sums * envelope * grad_scale
    grad_out_weight = jnp.dot(hidden_two.T, grad_taps, precision=FULL_PRECISION)
    unit_grad = lax.psum(
        jnp.dot(grad_taps, out_weight.T, precision=FULL_PRECISION).astype(jnp.bfloat16), "ch"
    ).astype(jnp.float32)
    grad_two = unit_grad * jnp.cos(pre_second)
    grad_second_weight = jnp.dot(hidden_one.T, grad_two, precision=FULL_PRECISION)
    grad_second_bias = jnp.sum(grad_two, axis=0)
    grad_one = jnp.dot(grad_two, second_weight.T, precision=FULL_PRECISION) * jnp.cos(pre_first)
    grad_first_weight = jnp.dot(features.T, grad_one, precision=FULL_PRECISION)
    grad_first_bias = jnp.sum(grad_one, axis=0)
    return (
        grad_inputs,
        grad_gates,
        grad_first_weight,
        grad_first_bias,
        grad_second_weight,
        grad_second_bias,
        grad_out_weight,
    )


MESH = pl.DeviceIdType.MESH


def bf(value):
    return value.astype(jnp.bfloat16)


def dot(left, right, dims=((1,), (0,)), precision=None):
    return lax.dot_general(
        left, right, (dims, ((), ())), precision=precision, preferred_element_type=jnp.float32
    )


def packed_table(tokens):
    half = tokens // 2
    freq = np.arange(half)[:, None]
    time = np.arange(tokens)[None, :]
    angles = 2.0 * np.pi / tokens * (freq * time % tokens)
    lower = -np.sin(angles)
    lower[0] = 1.0 - 2.0 * (np.arange(tokens) % 2)
    return np.concatenate([np.cos(angles), lower]).astype(np.float32)


def exchange_kernel(
    sizes, x_ref, gate_ref, gout_ref, w1_ref, b1_ref, w2_ref, b2_ref, decay_ref, mask_ref,
    feat_ref, featt_ref, table_hbm, ow_hbm,
    gi_ref, gg_ref, gw1_ref, gb1_ref, gw2_ref, gb2_ref, gow_ref,
    table, turned, ow, carried, xc, conv_in, taps, env, spec, tspec, prod, back, sums,
    gts, gtall, units, send_sem, recv_sem, usend, urecv, local_sem,
):
    n, m, rows, width, window, period = sizes
    tokens = n * rows
    half = tokens // 2
    me = lax.axis_index("seq")
    mine = lax.axis_index("ch")
    table_copy = pltpu.make_async_copy(table_hbm, table, local_sem.at[0])
    table_copy.start()
    ow_copy = pltpu.make_async_copy(ow_hbm, ow, local_sem.at[1])
    ow_copy.start()
    carried[...] = bf(gout_ref[...].astype(jnp.float32) * gate_ref[...].astype(jnp.float32))
    order = sorted(range(1, n), key=lambda step: -min(step, n - step))
    peers = {step: lax.rem(me + step, n) for step in order}
    others = {step: lax.rem(mine + step, m) for step in range(1, m)}

    barrier = pltpu.get_barrier_semaphore()
    for step in order:
        pl.semaphore_signal(barrier, inc=1, device_id={"seq": peers[step]}, device_id_type=MESH)
    for step in range(1, m):
        pl.semaphore_signal(barrier, inc=1, device_id={"ch": others[step]}, device_id_type=MESH)
    pl.semaphore_wait(barrier, n + m - 2)

    own_rows = pl.ds(pl.multiple_of(me * rows, rows), rows)
    own_cols = pl.ds(pl.multiple_of(me * width, width), width)

    def send(kind, step, source, target):
        copy = pltpu.make_async_remote_copy(
            src_ref=source, dst_ref=target,
            send_sem=send_sem.at[kind, step], recv_sem=recv_sem.at[kind, step],
            device_id={"seq": peers[step]}, device_id_type=MESH,
        )
        copy.start()
        return copy

    arriving = []
    for kind, source in ((0, x_ref), (1, carried)):
        for step in order:
            cols = pl.ds(pl.multiple_of(peers[step] * width, width), width)
            arriving.append(
                send(kind, step, source.at[:, cols], xc.at[own_rows, pl.ds(kind * width, width)])
            )
    xc[own_rows, 0:width] = x_ref[:, own_cols]
    xc[own_rows, width : 2 * width] = carried[:, own_cols]

    full = lax.Precision.HIGHEST
    pre_one = dot(feat_ref[...], w1_ref[...], precision=full) + b1_ref[...]
    h_one = jnp.sin(pre_one)
    slope_one = jnp.cos(pre_one)
    pre_two = dot(h_one, w2_ref[...], precision=full) + b2_ref[...]
    h_two = jnp.sin(pre_two)
    slope_two = jnp.cos(pre_two)
    ow_copy.wait()
    base = dot(h_two, ow[:, own_cols], precision=full)
    decay = decay_ref[:, own_cols]
    lengths = mask_ref[:, own_cols]
    for block in range(window // period):
        lag = lax.broadcasted_iota(jnp.int32, (period, width), 0) + block * period
        part = jnp.where(lag < lengths, jnp.exp(-decay * lag.astype(jnp.float32)), 0.0)
        env[pl.ds(block * period, period), :] = part
        taps[pl.ds(block * period, period), :] = bf(base * part)
    table_copy.wait()

    @pl.loop(0, tokens // 256)
    def _(i):
        piece = pl.ds(pl.multiple_of(i * 256, 256), 256)
        tspec[piece, :] = dot(table[piece, 0:window], taps[...])
        turned[:, piece] = table[piece, :].T

    h_one_t = bf(h_one.T)
    h_two_t = bf(h_two.T)
    for copy in arriving:
        copy.wait()

    @pl.loop(0, tokens // 256)
    def _(i):
        piece = pl.ds(pl.multiple_of(i * 256, 256), 256)
        spec[piece, :] = dot(table[piece, :], xc[...])

    @pl.loop(0, half // 64)
    def _(i):
        upper = pl.ds(pl.multiple_of(i * 64, 64), 64)
        lower = pl.ds(pl.multiple_of(half + i * 64, 64), 64)
        first = (lax.broadcasted_iota(jnp.int32, (64, width), 0) + i * 64) == 0
        weight = jnp.where(first, 1.0 / tokens, 2.0 / tokens)
        xr, xi = spec[upper, 0:width], spec[lower, 0:width]
        cr, ci = spec[upper, width : 2 * width], spec[lower, width : 2 * width]
        hr, hi = tspec[upper, :], tspec[lower, :]
        cx, hc, hx = ci * xi, hi * ci, hi * xi
        ts_r = cr * xr + jnp.where(first, 0.0, cx)
        ts_i = jnp.where(first, cx, ci * xr - cr * xi)
        gi_r = hr * cr + jnp.where(first, 0.0, hc)
        gi_i = jnp.where(first, hc, hr * ci - hi * cr)
        cv_r = hr * xr - jnp.where(first, 0.0, hx)
        cv_i = jnp.where(first, hx, hr * xi + hi * xr)
        for at, (real, imag) in enumerate(((ts_r, ts_i), (gi_r, gi_i), (cv_r, cv_i))):
            cols = slice(at * width, (at + 1) * width)
            prod[upper, cols] = bf(real * weight)
            prod[lower, cols] = bf(imag * weight)

    @pl.loop(0, window // 256)
    def _(i):
        piece = pl.ds(pl.multiple_of(i * 256, 256), 256)
        sums[piece, :] = dot(turned[piece, :], prod[:, 0:width])

    folded = sums[0:period, :] * env[0:period, :]
    for block in range(1, window // period):
        piece = pl.ds(block * period, period)
        folded = folded + sums[piece, :] * env[piece, :]
    folded = bf(folded * (1.0 / math.sqrt(tokens * window)))
    gts[...] = folded
    gtall[:, own_cols] = folded
    gathering = [send(2, step, gts, gtall.at[:, own_cols]) for step in order]

    @pl.loop(0, tokens // 256)
    def _(i):
        piece = pl.ds(pl.multiple_of(i * 256, 256), 256)
        back[piece, :] = bf(dot(turned[piece, :], prod[:, width : 3 * width]))

    returning = []
    for step in order:
        piece = pl.ds(pl.multiple_of(peers[step] * rows, rows), rows)
        returning.append(send(3, step, back.at[piece, pl.ds(0, width)], gi_ref.at[:, own_cols]))
        returning.append(
            send(4, step, back.at[piece, pl.ds(width, width)], conv_in.at[:, own_cols])
        )
    gi_ref[:, own_cols] = back[own_rows, 0:width]
    conv_in[:, own_cols] = back[own_rows, width : 2 * width]

    for copy in gathering:
        copy.wait()
    units[mine] = bf(dot(gtall[...], bf(ow[...]), ((1,), (1,))))
    crossing = []
    for step in range(1, m):
        copy = pltpu.make_async_remote_copy(
            src_ref=units.at[mine], dst_ref=units.at[mine],
            send_sem=usend.at[step], recv_sem=urecv.at[step],
            device_id={"ch": others[step]}, device_id_type=MESH,
        )
        copy.start()
        crossing.append(copy)
    gow_ref[...] = dot(h_two_t, gtall[...])
    for copy in crossing:
        copy.wait()
    unit = units[0].astype(jnp.float32)
    for other in range(1, m):
        unit = unit + units[other].astype(jnp.float32)
    grad_two = unit * slope_two
    gw2_ref[...] = dot(h_one_t, bf(grad_two))
    gb2_ref[...] = jnp.sum(grad_two, axis=0, keepdims=True)
    grad_one = dot(bf(grad_two), bf(w2_ref[...]), ((1,), (1,))) * slope_one
    gw1_ref[...] = dot(bf(featt_ref[...]), bf(grad_one))
    gb1_ref[...] = jnp.sum(grad_one, axis=0, keepdims=True)
    for copy in returning:
        copy.wait()
    gg_ref[...] = bf(gout_ref[...].astype(jnp.float32) * conv_in[...].astype(jnp.float32))


def exchanged(
    mesh_shape, inputs, gate_values, grad_out, first_weight, first_bias, second_weight,
    second_bias, out_weight, decay_rates, mask_lengths,
):
    n, m = mesh_shape["seq"], mesh_shape["ch"]
    rows, channels = inputs.shape
    width = channels // n
    window = SPAN * rows
    emb, units = first_weight.shape
    period = 2 * emb
    tokens = n * rows
    angles = (
        2.0 * np.pi / period
        * (np.arange(period)[:, None] * (np.arange(emb // 2)[None, :] + 1) % period)
    )
    features = np.concatenate([np.cos(angles), np.sin(angles)], axis=1).astype(np.float32)
    f32, b16 = jnp.float32, jnp.bfloat16
    vmem = pl.BlockSpec(memory_space=pltpu.VMEM)
    anywhere = pl.BlockSpec(memory_space=pl.ANY)
    shape = jax.ShapeDtypeStruct
    sem = pltpu.SemaphoreType.DMA
    outs = pl.pallas_call(
        functools.partial(exchange_kernel, (n, m, rows, width, window, period)),
        out_shape=(
            shape((rows, channels), b16), shape((rows, channels), b16),
            shape((emb, units), f32), shape((1, units), f32),
            shape((units, units), f32), shape((1, units), f32),
            shape((units, channels), f32),
        ),
        in_specs=[vmem] * 11 + [anywhere] * 2,
        out_specs=(vmem,) * 7,
        scratch_shapes=[
            pltpu.VMEM((tokens, tokens), b16), pltpu.VMEM((tokens, tokens), b16),
            pltpu.VMEM((units, channels), f32), pltpu.VMEM((rows, channels), b16),
            pltpu.VMEM((tokens, 2 * width), b16), pltpu.VMEM((rows, channels), b16),
            pltpu.VMEM((window, width), b16), pltpu.VMEM((window, width), f32),
            pltpu.VMEM((tokens, 2 * width), f32), pltpu.VMEM((tokens, width), f32),
            pltpu.VMEM((tokens, 3 * width), b16), pltpu.VMEM((tokens, 2 * width), b16),
            pltpu.VMEM((window, width), f32),
            pltpu.VMEM((period, width), b16), pltpu.VMEM((period, channels), b16),
            pltpu.VMEM((m, period, units), b16),
            sem((5, n)), sem((5, n)), sem((m,)), sem((m,)), sem((2,)),
        ],
        compiler_params=pltpu.CompilerParams(
            collective_id=0, has_side_effects=True, vmem_limit_bytes=48 * 1024 * 1024
        ),
        name="exchange",
    )(
        inputs, gate_values, grad_out, first_weight, first_bias[None], second_weight,
        second_bias[None], decay_rates[None], mask_lengths[None],
        jnp.asarray(features), jnp.asarray(features.T.copy()),
        jnp.asarray(packed_table(tokens), dtype=b16), out_weight,
    )
    grad_in, gates, gw1, gb1, gw2, gb2, gow = outs
    return grad_in, gates, gw1, gb1[0], gw2, gb2[0], gow


def solution(mesh):
    def body(*arrays):
        rows, channels = arrays[0].shape
        fits = channels == 128 * mesh.shape["seq"] and rows % 128 == 0
        if fits:
            return exchanged(mesh.shape, *arrays)
        return per_device(*arrays)

    in_specs = (
        P("seq", "ch"),
        P("seq", "ch"),
        P("seq", "ch"),
        P(),
        P(),
        P(),
        P(),
        P(None, "ch"),
        P("ch"),
        P("ch"),
    )
    out_specs = (P("seq", "ch"), P("seq", "ch"), P(), P(), P(), P(), P(None, "ch"))
    return jax.shard_map(
        body, mesh=mesh, in_specs=in_specs, out_specs=out_specs, check_vma=False
    )
```

```python
import math

import jax
import jax.numpy as jnp
import functools

import numpy as np
from jax import lax
from jax.experimental import pallas as pl
from jax.experimental.pallas import tpu as pltpu
from jax.sharding import PartitionSpec as P

SPAN = 4


FULL_PRECISION = lax.Precision.HIGHEST


def passed_along(value, axis, steps):
    count = lax.axis_size(axis)
    pairs = [(source, (source + steps) % count) for source in range(count)]
    return lax.ppermute(value, axis, pairs)


def angle_table(first_index, second_index, period):
    product = first_index[:, None] * second_index[None, :] % period
    return 2.0 * math.pi / period * product.astype(jnp.float32)


def lag_features(lag_count, feature_count):
    lag_index = jnp.arange(lag_count, dtype=jnp.int32)
    band_index = jnp.arange(feature_count // 2, dtype=jnp.int32) + 1
    phases = angle_table(lag_index, band_index, 2 * feature_count)
    return jnp.concatenate([jnp.cos(phases), jnp.sin(phases)], axis=1)


def split_table(table):
    upper_part = table.astype(jnp.bfloat16)
    lower_part = (table - upper_part.astype(jnp.float32)).astype(jnp.bfloat16)
    return (upper_part, lower_part)


def transform_tables(shard_rows):
    period = 2 * shard_rows
    frequency = jnp.arange(shard_rows + 1, dtype=jnp.int32)
    position = jnp.arange(shard_rows, dtype=jnp.int32)
    bin_weight = jnp.where((frequency == 0) | (frequency == shard_rows), 1.0, 2.0).astype(
        jnp.float32
    )
    forward_angles = angle_table(frequency, position, period)
    mirror_angles = angle_table(frequency, shard_rows - 1 - position, period)
    back_angles = angle_table(position + shard_rows, frequency, period)
    mirror_back = angle_table(2 * shard_rows - 1 - position, frequency, period)
    front_table = jnp.stack([jnp.cos(forward_angles), -jnp.sin(forward_angles)])
    mirror_table = jnp.stack([jnp.cos(mirror_angles), -jnp.sin(mirror_angles)])
    back_plain = jnp.stack([jnp.cos(back_angles), -jnp.sin(back_angles)]) / period
    back_table = back_plain * bin_weight[None, None, :]
    mirror_out = jnp.stack([jnp.cos(mirror_back), -jnp.sin(mirror_back)]) * (
        bin_weight[None, None, :] / period
    )
    fold_table = front_table * bin_weight[None, :, None]
    parity = (1.0 - 2.0 * (frequency % 2).astype(jnp.float32))[None, :, None]
    return (front_table, mirror_table, back_plain, back_table, mirror_out, fold_table, parity)


def spectrum(table_in, signal):
    return jnp.einsum("kfs,sc->kfc", table_in, signal, precision=FULL_PRECISION)


def sample_spectrum(table_pair, signal):
    upper_term = jnp.einsum(
        "kfs,sc->kfc", table_pair[0], signal, preferred_element_type=jnp.float32
    )
    lower_term = jnp.einsum(
        "kfs,sc->kfc", table_pair[1], signal, preferred_element_type=jnp.float32
    )
    return upper_term + lower_term


def sample_pullback(table_pair, signal):
    upper_term = jnp.einsum(
        "ksf,sc->kfc", table_pair[0], signal, preferred_element_type=jnp.float32
    )
    lower_term = jnp.einsum(
        "ksf,sc->kfc", table_pair[1], signal, preferred_element_type=jnp.float32
    )
    return upper_term + lower_term


def complex_product(left_factor, right_factor):
    real_part = left_factor[0] * right_factor[0] - left_factor[1] * right_factor[1]
    imag_part = left_factor[0] * right_factor[1] + left_factor[1] * right_factor[0]
    return jnp.stack([real_part, imag_part])


def conjugate_product(left_factor, right_factor):
    real_part = left_factor[0] * right_factor[0] + left_factor[1] * right_factor[1]
    imag_part = left_factor[1] * right_factor[0] - left_factor[0] * right_factor[1]
    return jnp.stack([real_part, imag_part])


def weighted_sum(filter_mixes, spectra_items):
    accumulated = complex_product(filter_mixes[0], spectra_items[0])
    for offset in range(1, len(filter_mixes)):
        accumulated = accumulated + complex_product(filter_mixes[offset], spectra_items[offset])
    return accumulated


def per_device(
    inputs,
    gate_values,
    grad_out,
    first_weight,
    first_bias,
    second_weight,
    second_bias,
    out_weight,
    decay_rates,
    mask_lengths,
):
    shard_rows = inputs.shape[0]
    window = SPAN * shard_rows
    front_table, mirror_table, back_plain, back_table, mirror_out, fold_table, parity = (
        transform_tables(shard_rows)
    )
    front_pair = split_table(front_table)
    mirror_pair = split_table(mirror_table)
    pull_pair = split_table(back_plain)
    features = lag_features(window, first_weight.shape[0])
    pre_first = jnp.dot(features, first_weight, precision=FULL_PRECISION) + first_bias
    hidden_one = jnp.sin(pre_first)
    pre_second = jnp.dot(hidden_one, second_weight, precision=FULL_PRECISION) + second_bias
    hidden_two = jnp.sin(pre_second)
    lag_index = jnp.arange(window, dtype=jnp.int32)
    envelope = jnp.exp(-decay_rates[None, :] * lag_index.astype(jnp.float32)[:, None]) * (
        lag_index[:, None] < mask_lengths[None, :]
    ).astype(jnp.float32)
    filter_taps = jnp.dot(hidden_two, out_weight, precision=FULL_PRECISION) * envelope
    block_spectra = [
        spectrum(front_table, filter_taps[block * shard_rows : (block + 1) * shard_rows])
        for block in range(SPAN)
    ]
    filter_mixes = []
    for offset in range(SPAN + 1):
        if offset == 0:
            mixed = parity * block_spectra[0]
        elif offset == SPAN:
            mixed = block_spectra[SPAN - 1]
        else:
            mixed = block_spectra[offset - 1] + parity * block_spectra[offset]
        filter_mixes.append(mixed)
    carried = (grad_out.astype(jnp.float32) * gate_values.astype(jnp.float32)).astype(jnp.bfloat16)
    earlier_spectra = [sample_spectrum(front_pair, inputs)]
    later_spectra = [sample_spectrum(mirror_pair, carried)]
    for offset in range(1, SPAN + 1):
        earlier = passed_along(inputs, "seq", offset)
        later = passed_along(carried, "seq", -offset)
        earlier_spectra.append(sample_spectrum(front_pair, earlier))
        later_spectra.append(sample_spectrum(mirror_pair, later))
    convolved = jnp.einsum(
        "ksf,kfc->sc",
        back_table,
        weighted_sum(filter_mixes, earlier_spectra),
        precision=FULL_PRECISION,
    )
    grad_gates = (grad_out.astype(jnp.float32) * convolved).astype(jnp.bfloat16)
    grad_inputs = jnp.einsum(
        "ksf,kfc->sc",
        mirror_out,
        weighted_sum(filter_mixes, later_spectra),
        precision=FULL_PRECISION,
    ).astype(jnp.bfloat16)
    pulled = sample_pullback(pull_pair, carried)
    grad_mixes = [conjugate_product(pulled, spectra_item) for spectra_item in earlier_spectra]
    pieces = []
    for block in range(SPAN):
        grad_block = parity * grad_mixes[block] + grad_mixes[block + 1]
        pieces.append(jnp.einsum("kfs,kfc->sc", fold_table, grad_block, precision=FULL_PRECISION))
    tap_terms = jnp.concatenate(pieces, axis=0)
    grad_scale = 1.0 / math.sqrt(lax.axis_size("seq") * shard_rows * window)
    tap_sums = lax.psum(tap_terms, "seq")
    grad_taps = tap_sums * envelope * grad_scale
    grad_out_weight = jnp.dot(hidden_two.T, grad_taps, precision=FULL_PRECISION)
    unit_grad = lax.psum(
        jnp.dot(grad_taps, out_weight.T, precision=FULL_PRECISION).astype(jnp.bfloat16), "ch"
    ).astype(jnp.float32)
    grad_two = unit_grad * jnp.cos(pre_second)
    grad_second_weight = jnp.dot(hidden_one.T, grad_two, precision=FULL_PRECISION)
    grad_second_bias = jnp.sum(grad_two, axis=0)
    grad_one = jnp.dot(grad_two, second_weight.T, precision=FULL_PRECISION) * jnp.cos(pre_first)
    grad_first_weight = jnp.dot(features.T, grad_one, precision=FULL_PRECISION)
    grad_first_bias = jnp.sum(grad_one, axis=0)
    return (
        grad_inputs,
        grad_gates,
        grad_first_weight,
        grad_first_bias,
        grad_second_weight,
        grad_second_bias,
        grad_out_weight,
    )


VMEM_LIMIT = 67_000_000
MESH = pl.DeviceIdType.MESH


def bf(value):
    return value.astype(jnp.bfloat16)


def dot(left, right, dims=((1,), (0,)), precision=None):
    return lax.dot_general(
        left, right, (dims, ((), ())), precision=precision, preferred_element_type=jnp.float32
    )


def packed_table(tokens):
    half = tokens // 2
    freq = np.arange(half)[:, None]
    time = np.arange(tokens)[None, :]
    angles = 2.0 * np.pi / tokens * (freq * time % tokens)
    lower = -np.sin(angles)
    lower[0] = 1.0 - 2.0 * (np.arange(tokens) % 2)
    return np.concatenate([np.cos(angles), lower]).astype(np.float32)


def exchange_kernel(
    sizes, x_hbm, gate_hbm, gout_hbm, w1_hbm, b1_hbm, w2_hbm, b2_hbm, decay_hbm, mask_hbm,
    feat_hbm, featt_hbm, ow_hbm, table_hbm,
    gi_out, gg_out, gw1_out, gb1_out, gw2_out, gb2_out, gow_out,
    gi_ref, gg_ref, gw1_ref, gb1_ref, gw2_ref, gb2_ref, gow_ref,
    x_ref, gate_ref, gout_ref, w1_ref, b1_ref, w2_ref, b2_ref, decay_ref, mask_ref,
    feat_ref, featt_ref, ow, table,
    ow_hi, ow_lo, turned, carried, xc, conv_in, taps, env, spec, tspec, prod, back, sums,
    gts, gtall, units, send_sem, recv_sem, usend, urecv, local_sem,
    store_sem,
):
    n, m, rows, width, window, period = sizes
    tokens = n * rows
    half = tokens // 2
    me = lax.axis_index("seq")
    mine = lax.axis_index("ch")
    loads = []
    for at, (source, target) in enumerate((
        (x_hbm, x_ref), (gate_hbm, gate_ref), (gout_hbm, gout_ref), (w1_hbm, w1_ref),
        (b1_hbm, b1_ref), (w2_hbm, w2_ref), (b2_hbm, b2_ref), (decay_hbm, decay_ref),
        (mask_hbm, mask_ref), (feat_hbm, feat_ref), (featt_hbm, featt_ref), (ow_hbm, ow),
        (table_hbm, table),
    )):
        load = pltpu.make_async_copy(source, target, local_sem.at[at])
        load.start()
        loads.append(load)
    order = sorted(range(1, n), key=lambda step: -min(step, n - step))
    peers = {step: lax.rem(me + step, n) for step in order}
    others = {step: lax.rem(mine + step, m) for step in range(1, m)}

    barrier = pltpu.get_barrier_semaphore()
    for step in order:
        pl.semaphore_signal(barrier, inc=1, device_id={"seq": peers[step]}, device_id_type=MESH)
    for step in range(1, m):
        pl.semaphore_signal(barrier, inc=1, device_id={"ch": others[step]}, device_id_type=MESH)
    for load in loads[:3]:
        load.wait()
    carried[...] = bf(gout_ref[...].astype(jnp.float32) * gate_ref[...].astype(jnp.float32))
    pl.semaphore_wait(barrier, n + m - 2)

    own_rows = pl.ds(pl.multiple_of(me * rows, rows), rows)
    own_cols = pl.ds(pl.multiple_of(me * width, width), width)

    def send(kind, step, source, target):
        copy = pltpu.make_async_remote_copy(
            src_ref=source, dst_ref=target,
            send_sem=send_sem.at[kind, step], recv_sem=recv_sem.at[kind, step],
            device_id={"seq": peers[step]}, device_id_type=MESH,
        )
        copy.start()
        return copy

    arriving = []
    for kind, source in ((0, x_ref), (1, carried)):
        for step in order:
            cols = pl.ds(pl.multiple_of(peers[step] * width, width), width)
            arriving.append(
                send(kind, step, source.at[:, cols], xc.at[own_rows, pl.ds(kind * width, width)])
            )
    xc[own_rows, 0:width] = x_ref[:, own_cols]
    xc[own_rows, width : 2 * width] = carried[:, own_cols]

    full = lax.Precision.HIGHEST
    for load in loads[3:]:
        load.wait()
    pre_one = dot(feat_ref[...], w1_ref[...], precision=full) + b1_ref[...]
    h_one = jnp.sin(pre_one)
    slope_one = jnp.cos(pre_one)
    pre_two = dot(h_one, w2_ref[...], precision=full) + b2_ref[...]
    h_two = jnp.sin(pre_two)
    slope_two = jnp.cos(pre_two)
    base = dot(h_two, ow[:, own_cols], precision=full)
    decay = decay_ref[:, own_cols]
    lengths = mask_ref[:, own_cols]
    for block in range(window // period):
        lag = lax.broadcasted_iota(jnp.int32, (period, width), 0) + block * period
        part = jnp.where(lag < lengths, jnp.exp(-decay * lag.astype(jnp.float32)), 0.0)
        env[pl.ds(block * period, period), :] = part
        taps[pl.ds(block * period, period), :] = bf(base * part)

    @pl.loop(0, tokens // 256)
    def _(i):
        piece = pl.ds(pl.multiple_of(i * 256, 256), 256)
        tspec[piece, :] = dot(table[piece, 0:window], taps[...])
        turned[:, piece] = table[piece, :].T

    h_one_t = h_one.T
    upper_ow = bf(ow[...])
    ow_hi[...] = upper_ow
    ow_lo[...] = bf(ow[...] - upper_ow.astype(jnp.float32))
    h_two_t = bf(h_two.T)
    for copy in arriving:
        copy.wait()

    @pl.loop(0, tokens // 256)
    def _(i):
        piece = pl.ds(pl.multiple_of(i * 256, 256), 256)
        spec[piece, :] = dot(table[piece, :], xc[...])

    @pl.loop(0, half // 64)
    def _(i):
        upper = pl.ds(pl.multiple_of(i * 64, 64), 64)
        lower = pl.ds(pl.multiple_of(half + i * 64, 64), 64)
        first = (lax.broadcasted_iota(jnp.int32, (64, width), 0) + i * 64) == 0
        weight = jnp.where(first, 1.0 / tokens, 2.0 / tokens)
        xr, xi = spec[upper, 0:width], spec[lower, 0:width]
        cr, ci = spec[upper, width : 2 * width], spec[lower, width : 2 * width]
        hr, hi = tspec[upper, :], tspec[lower, :]
        cx, hc, hx = ci * xi, hi * ci, hi * xi
        ts_r = cr * xr + jnp.where(first, 0.0, cx)
        ts_i = jnp.where(first, cx, ci * xr - cr * xi)
        gi_r = hr * cr + jnp.where(first, 0.0, hc)
        gi_i = jnp.where(first, hc, hr * ci - hi * cr)
        cv_r = hr * xr - jnp.where(first, 0.0, hx)
        cv_i = jnp.where(first, hx, hr * xi + hi * xr)
        for at, (real, imag) in enumerate(((ts_r, ts_i), (gi_r, gi_i), (cv_r, cv_i))):
            cols = slice(at * width, (at + 1) * width)
            prod[upper, cols] = bf(real * weight)
            prod[lower, cols] = bf(imag * weight)

    @pl.loop(0, window // 256)
    def _(i):
        piece = pl.ds(pl.multiple_of(i * 256, 256), 256)
        sums[piece, :] = dot(turned[piece, :], prod[:, 0:width])

    folded = sums[0:period, :] * env[0:period, :]
    for block in range(1, window // period):
        piece = pl.ds(block * period, period)
        folded = folded + sums[piece, :] * env[piece, :]
    folded = bf(folded * (1.0 / math.sqrt(tokens * window)))
    gts[...] = folded
    gtall[:, own_cols] = folded
    gathering = [send(2, step, gts, gtall.at[:, own_cols]) for step in order]

    @pl.loop(0, tokens // 256)
    def _(i):
        piece = pl.ds(pl.multiple_of(i * 256, 256), 256)
        back[piece, :] = bf(dot(turned[piece, :], prod[:, width : 3 * width]))

    returning = []
    for step in order:
        piece = pl.ds(pl.multiple_of(peers[step] * rows, rows), rows)
        returning.append(send(3, step, back.at[piece, pl.ds(0, width)], gi_ref.at[:, own_cols]))
        returning.append(
            send(4, step, back.at[piece, pl.ds(width, width)], conv_in.at[:, own_cols])
        )
    gi_ref[:, own_cols] = back[own_rows, 0:width]
    conv_in[:, own_cols] = back[own_rows, width : 2 * width]

    for copy in gathering:
        copy.wait()
    units[mine] = dot(gtall[...], ow_hi[...], ((1,), (1,))) + dot(
        gtall[...], ow_lo[...], ((1,), (1,))
    )
    crossing = []
    for step in range(1, m):
        copy = pltpu.make_async_remote_copy(
            src_ref=units.at[mine], dst_ref=units.at[mine],
            send_sem=usend.at[step], recv_sem=urecv.at[step],
            device_id={"ch": others[step]}, device_id_type=MESH,
        )
        copy.start()
        crossing.append(copy)
    gow_ref[...] = dot(h_two_t, gtall[...])
    stores = []

    def store(at, source, target):
        copy = pltpu.make_async_copy(source, target, store_sem.at[at])
        copy.start()
        stores.append(copy)

    store(0, gow_ref, gow_out)
    for copy in crossing:
        copy.wait()
    unit = units[0]
    for other in range(1, m):
        unit = unit + units[other]
    grad_two = unit * slope_two
    gw2_ref[...] = dot(h_one_t, grad_two, precision=full)
    gb2_ref[...] = jnp.sum(grad_two, axis=0, keepdims=True)
    grad_one = dot(grad_two, w2_ref[...], ((1,), (1,)), full) * slope_one
    gw1_ref[...] = dot(featt_ref[...], grad_one, precision=full)
    gb1_ref[...] = jnp.sum(grad_one, axis=0, keepdims=True)
    for at, (source, target) in enumerate((
        (gw2_ref, gw2_out), (gb2_ref, gb2_out), (gw1_ref, gw1_out), (gb1_ref, gb1_out)
    )):
        store(1 + at, source, target)
    for copy in returning:
        copy.wait()
    store(5, gi_ref, gi_out)
    gg_ref[...] = bf(gout_ref[...].astype(jnp.float32) * conv_in[...].astype(jnp.float32))
    store(6, gg_ref, gg_out)
    for copy in stores:
        copy.wait()


def drain_kernel(*refs):
    count = len(refs) // 3
    load_sem, store_sem = refs[-2:]
    loads = [
        pltpu.make_async_copy(refs[at], refs[2 * count + at], load_sem.at[at])
        for at in range(count)
    ]
    stores = [
        pltpu.make_async_copy(refs[2 * count + at], refs[count + at], store_sem.at[at])
        for at in range(count)
    ]
    for load in loads:
        load.start()
    for at in range(count):
        loads[at].wait()
        stores[at].start()
    for copy in stores:
        copy.wait()


def exchanged(
    mesh_shape, inputs, gate_values, grad_out, first_weight, first_bias, second_weight,
    second_bias, out_weight, decay_rates, mask_lengths,
):
    n, m = mesh_shape["seq"], mesh_shape["ch"]
    rows, channels = inputs.shape
    width = channels // n
    window = SPAN * rows
    emb, units = first_weight.shape
    period = 2 * emb
    tokens = n * rows
    angles = (
        2.0 * np.pi / period
        * (np.arange(period)[:, None] * (np.arange(emb // 2)[None, :] + 1) % period)
    )
    features = np.concatenate([np.cos(angles), np.sin(angles)], axis=1).astype(np.float32)
    f32, b16 = jnp.float32, jnp.bfloat16
    outside = pl.BlockSpec(memory_space=pltpu.HBM)
    shape = jax.ShapeDtypeStruct
    sem = pltpu.SemaphoreType.DMA
    arrays = (
        inputs, gate_values, grad_out, first_weight, first_bias[None], second_weight,
        second_bias[None], decay_rates[None], mask_lengths[None],
        jnp.asarray(features), jnp.asarray(features.T.copy()), out_weight,
        jnp.asarray(packed_table(tokens), dtype=b16),
    )
    out_shapes = (
        shape((rows, channels), b16), shape((rows, channels), b16),
        shape((emb, units), f32), shape((1, units), f32),
        shape((units, units), f32), shape((1, units), f32),
        shape((units, channels), f32),
    )
    outs = pl.pallas_call(
        functools.partial(exchange_kernel, (n, m, rows, width, window, period)),
        out_shape=out_shapes,
        in_specs=[outside] * 13,
        out_specs=(outside,) * 7,
        scratch_shapes=[
            *[pltpu.VMEM(out.shape, out.dtype) for out in out_shapes],
            *[pltpu.VMEM(array.shape, array.dtype) for array in arrays],
            pltpu.VMEM((units, channels), b16), pltpu.VMEM((units, channels), b16),
            pltpu.VMEM((tokens, tokens), b16), pltpu.VMEM((rows, channels), b16),
            pltpu.VMEM((tokens, 2 * width), b16), pltpu.VMEM((rows, channels), b16),
            pltpu.VMEM((window, width), b16), pltpu.VMEM((window, width), f32),
            pltpu.VMEM((tokens, 2 * width), f32), pltpu.VMEM((tokens, width), f32),
            pltpu.VMEM((tokens, 3 * width), b16), pltpu.VMEM((tokens, 2 * width), b16),
            pltpu.VMEM((window, width), f32),
            pltpu.VMEM((period, width), b16), pltpu.VMEM((period, channels), b16),
            pltpu.VMEM((m, period, units), f32),
            sem((5, n)), sem((5, n)), sem((m,)), sem((m,)), sem((13,)), sem((7,)),
        ],
        compiler_params=pltpu.CompilerParams(
            collective_id=0, has_side_effects=True, vmem_limit_bytes=VMEM_LIMIT
        ),
        name="exchange",
    )(*arrays)
    outs = pl.pallas_call(
        drain_kernel,
        out_shape=out_shapes,
        in_specs=[outside] * 7,
        out_specs=(outside,) * 7,
        scratch_shapes=[*[pltpu.VMEM(out.shape, out.dtype) for out in out_shapes], sem((7,)), sem((7,))],
        compiler_params=pltpu.CompilerParams(vmem_limit_bytes=VMEM_LIMIT),
        name="drain",
    )(*outs)
    grad_in, gates, gw1, gb1, gw2, gb2, gow = outs
    return grad_in, gates, gw1, gb1[0], gw2, gb2[0], gow


def solution(mesh):
    def body(*arrays):
        rows, channels = arrays[0].shape
        fits = channels == 128 * mesh.shape["seq"] and rows % 128 == 0
        if fits:
            return exchanged(mesh.shape, *arrays)
        return per_device(*arrays)

    in_specs = (
        P("seq", "ch"),
        P("seq", "ch"),
        P("seq", "ch"),
        P(),
        P(),
        P(),
        P(),
        P(None, "ch"),
        P("ch"),
        P("ch"),
    )
    out_specs = (P("seq", "ch"), P("seq", "ch"), P(), P(), P(), P(), P(None, "ch"))
    return jax.shard_map(
        body, mesh=mesh, in_specs=in_specs, out_specs=out_specs, check_vma=False
    )
```
